256 devices in a mesh: group: 4 (over x), owner: 64 (over z, y, core).
Axes of the slice: x: 4, y: 4, z: 8, core: 2. Of those that a mesh axis runs over, the one named last changes fastest.
Arguments:
- embeddings: bfloat16 [393216, 1024], P(('group', 'owner')), may hold values from -40 to 40
- assignment: int32 [393216, 1], P(('group', 'owner')), may hold values from 0 to 255, as said below
- home_map: int32 [256], replicated, may hold values from 0 to 255, each once
Outputs:
- centroids: float32 [256, 1024], P('owner')
- nearest: float32 [393216], P(('group', 'owner'))
- centrality: float32 [393216], P(('group', 'owner'))
The draws below stay inside these ranges and needn't reach their ends.
Inputs may be any that keep to these rules, and one draw needn't show every extreme that they name: `assignment`: in the rows of one device no cluster id occurs more than 12 times; the same quarter of the clusters occurs exactly 12 times in every device's rows. `home_map`: each home slot once.
All inputs are finite; a program needn't handle non-finite values.
Results may differ from the reference program's by a relative error of at most 0.00048.
Values may be sent and summed in bfloat16 or wider, within the bound.
A program may use at most 64 MiB of HBM per device.

```python
import jax
import jax.numpy as jnp
from jax import lax

D = 1024
CLUSTERS = 256
CAP = 12
ROWS_DEV = 1536
ROWS = 393216
N_GROUP = 4
N_OWNER = 64


def assign_clusters(key):
    position_member_tally = CLUSTERS * CAP
    block_total = ROWS // ROWS_DEV
    cluster_order = jax.random.permutation(jax.random.fold_in(key, 101), CLUSTERS)
    frequent_group_choice = (cluster_order % 4 == 0).astype(jnp.int32)
    position_group_number = jnp.arange(position_member_tally, dtype=jnp.int32) // CAP
    position_added_reward = frequent_group_choice[position_group_number]

    def one_block(block_key):
        small_perturbation = jax.random.randint(jax.random.fold_in(block_key, 1), (position_member_tally,), 0, 4096)
        angle_similarity_grid = (position_added_reward * 4096 + small_perturbation) * position_member_tally + jnp.arange(position_member_tally, dtype=jnp.int32)
        chosen = jnp.argsort(-angle_similarity_grid)[:ROWS_DEV]
        picked = position_group_number[chosen]
        return jax.random.permutation(jax.random.fold_in(block_key, 2), picked)
    block_keys = jax.random.split(jax.random.fold_in(key, 202), block_total)
    return jax.vmap(one_block)(block_keys).reshape(ROWS, 1).astype(jnp.int32)


def draw_assignment(key, part):
    return assign_clusters(key)


def draw_embeddings(key, part):
    cluster_ids = assign_clusters(key)[:, 0]
    centers = jax.random.normal(jax.random.fold_in(key, 303), (CLUSTERS, D), jnp.float32)
    small_perturbation = jax.random.normal(jax.random.fold_in(key, 404), (ROWS, D), jnp.float32)
    values = centers[cluster_ids] + small_perturbation
    return jnp.clip(values, -40.0, 40.0).astype(jnp.bfloat16)


def setup_inputs(seed: int = 0) -> dict:
    splits = jax.random.split(jax.random.key(seed), 4)
    embeddings = draw_embeddings(jax.random.fold_in(splits[3], 71), 0)
    assignment = draw_assignment(jax.random.fold_in(splits[3], 71), 0)
    home_map = jax.random.permutation(splits[2], CLUSTERS).astype(jnp.int32)
    return dict(embeddings=embeddings, assignment=assignment, home_map=home_map)


def normalize_rows(descriptor_vectors):
    values = descriptor_vectors.astype(jnp.float32)
    return values * lax.rsqrt(lax.optimization_barrier(jnp.mean(values * values, axis=-1, keepdims=True)) + 1e-06)

def rank_within(cluster_ids):
    positions = jnp.arange(cluster_ids.shape[0], dtype=jnp.int32)
    earlier = (cluster_ids[:, None] == cluster_ids[None, :]) & (positions[:, None] > positions[None, :])
    return lax.optimization_barrier(jnp.sum(earlier.astype(jnp.int32), axis=1)).astype(jnp.int32)

def reference(embeddings, assignment, home_map):
    normed = normalize_rows(embeddings).astype(jnp.bfloat16)
    cluster_ids = assignment[:, 0].astype(jnp.int32)
    home_slot = home_map[cluster_ids].astype(jnp.int32)
    cluster_totals = jax.ops.segment_sum(normed.astype(jnp.float32), home_slot, num_segments=CLUSTERS)
    centroids = normalize_rows(cluster_totals)
    centroid_low = centroids.astype(jnp.bfloat16)

    def central_block(packed_pair):
        row_block, device_homes = packed_pair
        picked = centroid_low[device_homes]
        return lax.optimization_barrier(jnp.sum(row_block.astype(jnp.float32) * picked.astype(jnp.float32), axis=-1)) / D
    by_device = normed.reshape(N_GROUP * N_OWNER, ROWS_DEV, D)
    homes_by_device = home_slot.reshape(N_GROUP * N_OWNER, ROWS_DEV)
    centrality = lax.map(central_block, (by_device, homes_by_device)).reshape(-1)
    all_ranks = lax.map(rank_within, cluster_ids.reshape(N_GROUP * N_OWNER, ROWS_DEV))
    source_identity_matrix = jnp.eye(N_OWNER, dtype=jnp.bool_)
    slot_eye = jnp.eye(CAP, dtype=jnp.bool_)
    self_pair = source_identity_matrix[:, None, :, None] & slot_eye[None, :, None, :]

    def cluster_scores(cluster_block):
        member_block, mark_block = cluster_block
        values = member_block.astype(jnp.float32)
        similarity = jnp.einsum('spd,tqd->sptq', values, values) / D
        allowed = (mark_block[None, None, :, :] > 0) & ~self_pair
        return lax.optimization_barrier(jnp.max(jnp.where(allowed, similarity, -1.0), axis=(2, 3)))

    def group_scores(packed_group):
        row_group, group_homes, group_ranks = packed_group
        input_samples = jnp.broadcast_to(jnp.arange(N_OWNER, dtype=jnp.int32)[:, None], group_homes.shape)
        layout = jnp.zeros((CLUSTERS, N_OWNER, CAP, D), jnp.bfloat16).at[group_homes, input_samples, group_ranks].set(row_group)
        present = jnp.zeros((CLUSTERS, N_OWNER, CAP), jnp.float32).at[group_homes, input_samples, group_ranks].set(1.0)
        best_scores = lax.map(cluster_scores, (layout, present))
        return best_scores[group_homes, input_samples, group_ranks]
    nearest = lax.map(group_scores, (normed.reshape(N_GROUP, N_OWNER, ROWS_DEV, D), home_slot.reshape(N_GROUP, N_OWNER, ROWS_DEV), all_ranks.reshape(N_GROUP, N_OWNER, ROWS_DEV))).reshape(-1)
    return (centroids, nearest, centrality)
```

```python
import functools

import jax
import jax.numpy as jnp
from jax import lax
from jax.experimental import pallas as pl
from jax.experimental.pallas import tpu as pltpu
from jax.sharding import PartitionSpec as P

MESH = pl.DeviceIdType.MESH
F32 = jnp.float32
BF16 = jnp.bfloat16
I32 = jnp.int32

NZ, NY, NC = 8, 4, 2
NW = NY * NC
NX = 4
PLANE = 32
RANKS = 16
MARK = 128.0
NEG = -1e30
EPS = 1e-06


def dot(a, b):
    return lax.dot_general(a, b, (((1,), (0,)), ((), ())), preferred_element_type=F32)


def dot_t(a, b):
    return lax.dot_general(a, b, (((1,), (1,)), ((), ())), preferred_element_type=F32)


def iota(shape, axis):
    return lax.broadcasted_iota(I32, shape, axis)


def hot(mask):
    return jnp.where(mask, 1.0, 0.0).astype(BF16)


def z_order(i):
    return jnp.where(lax.rem(i, 2) == 0, 1 + i // 2, NZ - 1 - i // 2)


def kernel(cap, emb, ids, hm, cent_o, near_o, central_o, flag_o,
           normed, buf, meta, stage, mem, info, val, acc, flags, xbuf, near, ret, rz, rp, on_s, oc_s,
           zss, zrs, mss, mrs, iss, irs, xss, xrs, rss, rrs, pss, prs):
    rows, feat = emb.shape
    clusters = hm.shape[1]
    gx = lax.axis_index("group")
    me = lax.axis_index("owner")
    z, y, c = me // NW, lax.rem(me // NC, NY), lax.rem(me, NC)

    def z_dev(d):
        return lax.rem(z + d + NZ, NZ) * NW + y * NC + c

    def w_dev(e, sign):
        dy, dc = e // NC, lax.rem(e, NC)
        return z * NW + lax.rem(y + sign * dy + NY, NY) * NC + lax.rem(c + dc, NC)

    barrier = pltpu.get_barrier_semaphore()
    for d in range(1, NZ):
        pl.semaphore_signal(barrier, inc=1, device_id={"owner": z_dev(d)}, device_id_type=MESH)
    for e in range(1, NW):
        pl.semaphore_signal(barrier, inc=1, device_id={"owner": w_dev(e, 1)}, device_id_type=MESH)
    for k in range(1, NX):
        pl.semaphore_signal(barrier, inc=1, device_id={"group": lax.rem(gx + k, NX)}, device_id_type=MESH)

    h = hm[...]
    rel = (((h // PLANE - z + NZ) % NZ) * PLANE + ((h // 8 % NY - y + NY) % NY) * 8
           + ((h // 4 % NC + c) % NC) * 4 + h % 4)
    perm = hot(iota((clusters, clusters), 0) == rel)
    home = dot(perm, hot(iota((clusters, rows), 0) == ids[...])).astype(BF16)
    before = hot(iota((256, 256), 0) < iota((256, 256), 1))
    same = hot(iota((clusters, clusters), 0) // PLANE == iota((clusters, clusters), 1) // PLANE)
    base = jnp.zeros((clusters, 1), F32)
    number = iota((clusters, 256), 0).astype(F32)
    for k in range(rows // 256):
        part = home[:, k * 256:(k + 1) * 256]
        count = dot(part, before) + base
        wide = part.astype(F32)
        lanes = pl.ds(k * 256, 256)
        info[0:1, lanes] = jnp.sum(wide * number, axis=0, keepdims=True)
        info[1:2, lanes] = jnp.sum(wide * count, axis=0, keepdims=True)
        info[2:3, lanes] = jnp.sum(dot(same, part) * count, axis=0, keepdims=True)
        base = base + jnp.sum(wide, axis=1, keepdims=True)
    rel_home = info[0:1, :].astype(I32)
    rank = info[1:2, :]
    place = info[2:3, :]
    plane = rel_home // PLANE
    target = jnp.where(place < cap, plane * cap + place.astype(I32), -1)
    info[3:4, :] = target.astype(F32)
    over = jnp.where(jnp.max(place, axis=1, keepdims=True) >= cap, 1.0, 0.0)
    low = (rel_home - plane * PLANE + 1).astype(F32)
    row_of = iota((16, rows), 0)
    val[...] = jnp.where(row_of == 0, low, jnp.where(row_of == 1, rank, 0.0)).astype(BF16)

    for k in range(rows // 256):
        x = emb[pl.ds(k * 256, 256), :].astype(F32)
        scale = lax.rsqrt(jnp.mean(x * x, axis=-1, keepdims=True) + EPS)
        normed[pl.ds(k * 256, 256), :] = (x * scale).astype(BF16)
    meta[0:NZ] = jnp.zeros((NZ,) + meta.shape[1:], F32)

    pl.semaphore_wait(barrier, NZ - 1 + NW - 1 + NX - 1)

    def z_copy(d):
        return pltpu.make_async_remote_copy(
            src_ref=buf.at[d], dst_ref=buf.at[NZ + d], send_sem=zss.at[d], recv_sem=zrs.at[d],
            device_id={"owner": z_dev(d)}, device_id_type=MESH)

    def m_copy(d):
        return pltpu.make_async_remote_copy(
            src_ref=meta.at[d], dst_ref=meta.at[NZ + d], send_sem=mss.at[d], recv_sem=mrs.at[d],
            device_id={"owner": z_dev(d)}, device_id_type=MESH)

    def i_copy(d, e):
        return pltpu.make_async_remote_copy(
            src_ref=stage.at[d, e], dst_ref=mem.at[:, d, e], send_sem=iss.at[d, e], recv_sem=irs.at[d, e],
            device_id={"owner": w_dev(e, 1)}, device_id_type=MESH)

    def send_plane(i, _):
        d = jnp.where(i == NZ - 1, 0, z_order(i))
        pick = hot(iota((cap, rows), 0) + d * cap == info[3:4, :].astype(I32))
        buf[d] = dot(pick, normed[...]).astype(BF16)
        notes = dot_t(val[...], pick)[0:8]
        meta[d, :, 0:cap] = jnp.where(iota((8, cap), 0) == 2, over, notes)

        @pl.when(i < NZ - 1)
        def _():
            m_copy(d).start()
            z_copy(d).start()
        return 0

    lax.fori_loop(0, NZ, send_plane, 0)

    line = iota((NW * NZ * 8, 1), 0)
    v = line % 8
    code = (line // 8 % NZ) * PLANE + (line // 64) * 4
    on_s[...] = hot(jnp.where(v < 4, code + v, -1) == info[0:1, :].astype(I32))
    oc_s[...] = hot(jnp.where(v >= 4, code + v - 4, -1) == info[0:1, :].astype(I32))
    acc[...] = jnp.zeros_like(acc)
    flags[...] = jnp.zeros_like(flags)
    first = hot((iota((16, 128), 1) == 0))

    def step(j, _):
        @pl.when(j < NZ)
        def _():
            d = jnp.where(j == 0, 0, z_order(j - 1))

            @pl.when(j > 0)
            def _():
                m_copy(d).wait_recv()
                z_copy(d).wait_recv()
            slot = jnp.where(j == 0, 0, NZ + d)
            notes = meta[slot]
            q = ((notes[0:1, 0:cap] - 1.0) * RANKS + notes[1:2, 0:cap]).astype(I32)
            mark = MARK + MARK * jnp.max(notes[2:3, :], axis=1, keepdims=True)
            spread = jnp.where(iota((NW * 64, cap), 0) == q, 1.0, 0.0)
            absent = 1.0 - jnp.sum(spread, axis=1, keepdims=True)
            out = dot(spread.astype(BF16), buf[slot])
            head = out[:, 0:128] + jnp.where(iota((NW * 64, 128), 1) == 0, absent * mark, 0.0)
            stage[d, :, :, :, 0:128] = head.astype(BF16).reshape(NW, 4, RANKS, 128)
            stage[d, :, :, :, 128:] = out[:, 128:].astype(BF16).reshape(NW, 4, RANKS, feat - 128)
            mem[:, d, 0] = stage[d, 0]
            for e in range(1, NW):
                i_copy(d, e).start()

        @pl.when(j > 0)
        def _():
            d = jnp.where(j == 1, 0, z_order(j - 2))
            for e in range(1, NW):
                i_copy(d, e).wait_recv()
            for k in range(4):
                block = mem[k, d].reshape(NW * RANKS, feat)
                lead = dot_t(first, block[:, 0:128])
                flags[...] = jnp.maximum(flags[...], lead)
                acc[k] += dot(hot(lead < 64.0), block)
        return 0

    lax.fori_loop(0, NZ + 1, step, 0)

    xbuf[gx] = jnp.zeros((8, feat), F32)
    for k in range(4):
        xbuf[gx, k:k + 1, :] = acc[k, 0:1, :]
    top = jnp.max(jnp.max(flags[...], axis=0, keepdims=True), axis=1, keepdims=True)
    xbuf[gx, 4:5, :] = jnp.broadcast_to(jnp.where(top > 1.5 * MARK, 1.0, 0.0), (1, feat))

    def x_copy(k):
        return pltpu.make_async_remote_copy(
            src_ref=xbuf.at[gx], dst_ref=xbuf.at[gx], send_sem=xss.at[k], recv_sem=xrs.at[k],
            device_id={"group": lax.rem(gx + k, NX)}, device_id_type=MESH)

    def x_arrival(k):
        return pltpu.make_async_remote_copy(
            src_ref=xbuf.at[gx], dst_ref=xbuf.at[lax.rem(gx - k + NX, NX)], send_sem=xss.at[k], recv_sem=xrs.at[k],
            device_id={"group": lax.rem(gx + k, NX)}, device_id_type=MESH)

    for k in range(1, NX):
        x_copy(k).start()

    n = NZ * NW * RANKS

    def score(i, _):
        k, jb = i // 4, lax.rem(i, 4)
        every = mem[k].reshape(n, feat)
        some = mem[k, pl.ds(jb * 2, 2)].reshape(256, feat)
        s = dot_t(every, some)
        gone = every[:, 0:128].astype(F32)[:, 0:1] > 64.0
        s = s + jnp.where(gone, NEG, 0.0)
        s = jnp.where(iota((n, 256), 0) == jb * 256 + iota((n, 256), 1), NEG, s)
        best = jnp.maximum(jnp.max(s, axis=0, keepdims=True) * (1.0 / feat), -1.0)
        near[k, jb * 2] = best[:, 0:128]
        near[k, jb * 2 + 1] = best[:, 128:256]
        return 0

    lax.fori_loop(0, 16, score, 0)

    for k in range(1, NX):
        x_arrival(k).wait_recv()
    totals = ((xbuf[0] + xbuf[1]) + xbuf[2]) + xbuf[3]
    centroids = totals * lax.rsqrt(jnp.mean(totals * totals, axis=-1, keepdims=True) + EPS)
    cent_o[...] = centroids[0:4]
    flag_o[...] = jnp.broadcast_to(totals[4:5, 0:128], (8, 128))
    lowc = jnp.concatenate([centroids, centroids], axis=0).astype(BF16)
    for k in range(4):
        central = dot_t(lowc, mem[k].reshape(n, feat)) * (1.0 / feat)
        for d in range(NZ):
            ret[d, k:k + 1, :] = near[k, d]
            ret[d, 4 + k:5 + k, :] = central[k:k + 1, d * 128:(d + 1) * 128]

    def r_copy(d):
        return pltpu.make_async_remote_copy(
            src_ref=ret.at[d], dst_ref=rz.at[d], send_sem=rss.at[d], recv_sem=rrs.at[d],
            device_id={"owner": z_dev(-d)}, device_id_type=MESH)

    def p_copy(e):
        return pltpu.make_async_remote_copy(
            src_ref=rz, dst_ref=rp.at[e], send_sem=pss.at[e], recv_sem=prs.at[e],
            device_id={"owner": w_dev(e, -1)}, device_id_type=MESH)

    for d in range(1, NZ):
        r_copy(d).start()
    rz[0] = ret[0]
    for d in range(1, NZ):
        r_copy(d).wait_recv()
    for e in range(1, NW):
        p_copy(e).start()
    rp[0] = rz[...]
    for e in range(1, NW):
        p_copy(e).wait_recv()

    back = rp[...].reshape(NW * NZ * 8, 128).T
    high = back.astype(BF16)
    both = jnp.concatenate([high, (back - high.astype(F32)).astype(BF16)], axis=0)
    rel_home = info[0:1, :].astype(I32)
    lane = (rel_home % PLANE) // 4 * RANKS + info[1:2, :].astype(I32)
    mine = iota((128, rows), 0) == lane
    for table, out_ref in ((on_s, near_o), (oc_s, central_o)):
        got = dot(both, table[...])
        got = got[0:128] + got[128:256]
        out_ref[...] = jnp.sum(jnp.where(mine, got, 0.0), axis=0, keepdims=True)

    for d in range(1, NZ):
        m_copy(d).wait_send()
        z_copy(d).wait_send()
        r_copy(d).wait_send()
    for e in range(1, NW):
        p_copy(e).wait_send()
    for k in range(1, NX):
        x_copy(k).wait_send()

    def drain(d, _):
        for e in range(1, NW):
            i_copy(d, e).wait_send()
        return 0

    lax.fori_loop(0, NZ, drain, 0)


def window(cap, collective_id, embeddings, ids, home_map):
    rows, feat = embeddings.shape
    dma = pltpu.SemaphoreType.DMA
    lanes = -(-cap // 128) * 128
    vmem = pl.BlockSpec(memory_space=pltpu.VMEM)
    cent, near, central, flag = pl.pallas_call(
        functools.partial(kernel, cap),
        out_shape=(
            jax.ShapeDtypeStruct((4, feat), F32),
            jax.ShapeDtypeStruct((1, rows), F32),
            jax.ShapeDtypeStruct((1, rows), F32),
            jax.ShapeDtypeStruct((8, 128), F32),
        ),
        in_specs=[vmem] * 3,
        out_specs=(vmem,) * 4,
        scratch_shapes=[
            pltpu.VMEM((rows, feat), BF16),
            pltpu.VMEM((2 * NZ, cap, feat), BF16),
            pltpu.VMEM((2 * NZ, 8, lanes), F32),
            pltpu.VMEM((NZ, NW, 4, RANKS, feat), BF16),
            pltpu.VMEM((4, NZ, NW, RANKS, feat), BF16),
            pltpu.VMEM((8, rows), F32),
            pltpu.VMEM((16, rows), BF16),
            pltpu.VMEM((4, 16, feat), F32),
            pltpu.VMEM((16, 128), F32),
            pltpu.VMEM((NX, 8, feat), F32),
            pltpu.VMEM((4, NZ, 1, 128), F32),
            pltpu.VMEM((NZ, 8, 128), F32),
            pltpu.VMEM((NZ, 8, 128), F32),
            pltpu.VMEM((NW, NZ, 8, 128), F32),
            pltpu.VMEM((NW * NZ * 8, rows), BF16),
            pltpu.VMEM((NW * NZ * 8, rows), BF16),
            dma((NZ,)), dma((NZ,)), dma((NZ,)), dma((NZ,)),
            dma((NZ, NW)), dma((NZ, NW)),
            dma((NX,)), dma((NX,)), dma((NZ,)), dma((NZ,)), dma((NW,)), dma((NW,)),
        ],
        compiler_params=pltpu.CompilerParams(
            collective_id=collective_id, has_side_effects=True, vmem_limit_bytes=62 * 1024 * 1024),
    )(embeddings, ids, home_map)
    return cent, near.reshape(-1), central.reshape(-1), flag


def body(embeddings, assignment, home_map):
    ids = assignment.reshape(1, -1)
    table = home_map.reshape(1, -1)
    cent, near, central, flag = window(288, 0, embeddings, ids, table)
    return lax.cond(
        flag[0, 0] > 0.5,
        lambda e, i, t, *_: window(384, 1, e, i, t)[:3],
        lambda e, i, t, *done: done,
        embeddings, ids, table, cent, near, central)


def solution(mesh):
    in_specs = (P(("group", "owner"), None), P(("group", "owner"), None), P())
    out_specs = (P("owner", None), P(("group", "owner")), P(("group", "owner")))
    return jax.shard_map(body, mesh=mesh, in_specs=in_specs, out_specs=out_specs, check_vma=False)
```

```python
import functools

import jax
import jax.numpy as jnp
from jax import lax
from jax.experimental import pallas as pl
from jax.experimental.pallas import tpu as pltpu
from jax.sharding import PartitionSpec as P

MESH = pl.DeviceIdType.MESH
F32 = jnp.float32
BF16 = jnp.bfloat16
I32 = jnp.int32

NZ, NY, NC = 8, 4, 2
NW = NY * NC
NX = 4
PLANE = 32
RANKS = 16
MARK = 128.0
NEG = -1e30
EPS = 1e-06
HALVES = 2
CAP = 272


def dot(a, b):
    return lax.dot_general(a, b, (((1,), (0,)), ((), ())), preferred_element_type=F32)


def dot_t(a, b):
    return lax.dot_general(a, b, (((1,), (1,)), ((), ())), preferred_element_type=F32)


def iota(shape, axis):
    return lax.broadcasted_iota(I32, shape, axis)


def hot(mask):
    return jnp.where(mask, 1.0, 0.0).astype(BF16)


def z_of(j):
    return jnp.where(lax.rem(j, 2) == 1, (j + 1) // 2, NZ - j // 2)


def kernel(cap, emb_hbm, ids, hm, cent_o, near_o, central_o, flag_o,
           emb, buf, meta, stage, mem, info, val, acc, flags, xbuf, near, ret, rz, pk, rp, on_s, oc_s,
           esem, zss, zrs, mss, mrs, iss, irs, xss, xrs, rss, rrs, pss, prs):
    rows, feat = emb.shape
    half = feat // HALVES
    clusters = hm.shape[1]
    gx = lax.axis_index("group")
    me = lax.axis_index("owner")
    z, y, c = me // NW, lax.rem(me // NC, NY), lax.rem(me, NC)

    def z_dev(j, sign=1):
        return lax.rem(z + sign * z_of(j) + NZ, NZ) * NW + y * NC + c

    def w_dev(e, sign):
        dy, dc = e // NC, lax.rem(e, NC)
        return z * NW + lax.rem(y + sign * dy + NY, NY) * NC + lax.rem(c + dc, NC)

    barrier = pltpu.get_barrier_semaphore()
    for j in range(1, NZ):
        pl.semaphore_signal(barrier, inc=1, device_id={"owner": z_dev(j)}, device_id_type=MESH)
    for e in range(1, NW):
        pl.semaphore_signal(barrier, inc=1, device_id={"owner": w_dev(e, 1)}, device_id_type=MESH)
    for k in range(1, NX):
        pl.semaphore_signal(barrier, inc=1, device_id={"group": lax.rem(gx + k, NX)}, device_id_type=MESH)
    load = pltpu.make_async_copy(emb_hbm, emb, esem)
    load.start()

    h = hm[...]
    dz = ((h >> 5) - z) & (NZ - 1)
    jz = jnp.where(dz == 0, 0, jnp.where(dz <= NZ // 2, 2 * dz - 1, 2 * (NZ - dz)))
    rel = (jz << 5) + ((((h >> 3) - y) & (NY - 1)) << 3) + ((((h >> 2) - c) & 1) << 2) + (h & 3)
    perm = hot(iota((clusters, clusters), 0) == rel)
    home = dot(perm, hot(iota((clusters, rows), 0) == ids[...])).astype(BF16)
    before = hot(iota((256, 256), 0) < iota((256, 256), 1))
    same = hot((iota((clusters, clusters), 0) >> 5) == (iota((clusters, clusters), 1) >> 5))
    base = jnp.zeros((clusters, 1), F32)
    number = iota((clusters, 256), 0).astype(F32)
    for k in range(rows // 256):
        part = home[:, k * 256:(k + 1) * 256]
        count = dot(part, before) + base
        wide = part.astype(F32)
        lanes = pl.ds(k * 256, 256)
        info[0:1, lanes] = jnp.sum(wide * number, axis=0, keepdims=True)
        info[1:2, lanes] = jnp.sum(wide * count, axis=0, keepdims=True)
        info[2:3, lanes] = jnp.sum(dot(same, part) * count, axis=0, keepdims=True)
        base = base + jnp.sum(wide, axis=1, keepdims=True)
    rel_home = info[0:1, :].astype(I32)
    rank = info[1:2, :]
    place = info[2:3, :]
    plane = rel_home >> 5
    low = rel_home & (PLANE - 1)
    info[3:4, :] = jnp.where(place < cap, plane * cap + place.astype(I32), -1).astype(F32)
    over = jnp.where(jnp.max(place, axis=1, keepdims=True) >= cap, 1.0, 0.0)
    row_of = iota((16, rows), 0)
    val[...] = jnp.where(row_of == 0, (low + 1).astype(F32), jnp.where(row_of == 1, rank, 0.0)).astype(BF16)
    lanes = meta.shape[2]
    if lanes > cap:
        meta[0:NZ] = jnp.zeros((NZ, 8, lanes), F32)

    pl.semaphore_wait(barrier, NZ - 1 + NW - 1 + NX - 1)
    load.wait()

    def z_copy(j, f):
        return pltpu.make_async_remote_copy(
            src_ref=buf.at[j, f], dst_ref=buf.at[NZ + j, f], send_sem=zss.at[j, f], recv_sem=zrs.at[j, f],
            device_id={"owner": z_dev(j)}, device_id_type=MESH)

    def m_copy(j):
        return pltpu.make_async_remote_copy(
            src_ref=meta.at[j], dst_ref=meta.at[NZ + j], send_sem=mss.at[j], recv_sem=mrs.at[j],
            device_id={"owner": z_dev(j)}, device_id_type=MESH)

    def i_copy(j, f, e):
        return pltpu.make_async_remote_copy(
            src_ref=stage.at[j, f, e], dst_ref=mem.at[:, j, e, :, pl.ds(f * half, half)],
            send_sem=iss.at[j, f, e], recv_sem=irs.at[j, f, e],
            device_id={"owner": w_dev(e, 1)}, device_id_type=MESH)

    def send_plane(i, _):
        j = lax.rem(i + 1, NZ)
        pick = hot(iota((cap, rows), 0) + j * cap == info[3:4, :].astype(I32))
        x = dot(pick, emb[...])
        x = x * lax.rsqrt(jnp.mean(x * x, axis=-1, keepdims=True) + EPS)
        for f in range(HALVES):
            buf[j, f] = x[:, f * half:(f + 1) * half].astype(BF16)
        notes = dot_t(val[...], pick)[0:8]
        meta[j, :, 0:cap] = jnp.where(iota((8, cap), 0) == 2, over, notes)

        @pl.when(j > 0)
        def _():
            m_copy(j).start()
            for f in range(HALVES):
                z_copy(j, f).start()
        return 0

    lax.fori_loop(0, NZ, send_plane, 0)

    line = iota((128, 1), 0)
    v = line & 7
    code = (line >> 3) * 4
    low = info[0:1, :].astype(I32) & (PLANE - 1)
    on_s[...] = hot(jnp.where((v < 4) & (line < 64), code + v, -1) == low)
    oc_s[...] = hot(jnp.where((v >= 4) & (line < 64), code + v - 4, -1) == low)
    acc[...] = jnp.zeros_like(acc)
    flags[...] = jnp.zeros_like(flags)
    first = hot((iota((16, 128), 1) == 0))

    def collect(j):
        for e in range(1, NW):
            for f in range(HALVES):
                i_copy(j, f, e).wait_recv()
        for k in range(4):
            block = mem[k, j].reshape(NW * RANKS, feat)
            lead = dot_t(first, block[:, 0:128])
            flags[...] = jnp.maximum(flags[...], lead)
            acc[k] += dot(hot(lead < 64.0), block)

    def step(j, _):
        @pl.when(j > 0)
        def _():
            m_copy(j).wait_recv()
        slot = jnp.where(j == 0, 0, NZ + j)
        notes = meta[slot]
        q = ((notes[0:1, 0:cap] - 1.0) * RANKS + notes[1:2, 0:cap]).astype(I32)
        mark = MARK + MARK * jnp.max(notes[2:3, 0:cap], axis=1, keepdims=True)
        spread = jnp.where(iota((NW * 64, cap), 0) == q, 1.0, 0.0)
        absent = 1.0 - jnp.sum(spread, axis=1, keepdims=True)
        head = jnp.where(iota((NW * 64, 128), 1) == 0, absent * mark, 0.0)
        spread = spread.astype(BF16)
        for f in range(HALVES):
            @pl.when(j > 0)
            def _():
                z_copy(j, f).wait_recv()
            out = dot(spread, buf[slot, f])
            if f == 0:
                stage[j, f, :, :, :, 0:128] = (out[:, 0:128] + head).astype(BF16).reshape(NW, 4, RANKS, 128)
                stage[j, f, :, :, :, 128:] = out[:, 128:].astype(BF16).reshape(NW, 4, RANKS, half - 128)
            else:
                stage[j, f] = out.astype(BF16).reshape(NW, 4, RANKS, half)
            for e in range(1, NW):
                i_copy(j, f, e).start()
            mem[:, j, 0, :, f * half:(f + 1) * half] = stage[j, f, 0]

        @pl.when(j > 0)
        def _():
            collect(j - 1)
        return 0

    lax.fori_loop(0, NZ, step, 0)

    n = NZ * NW * RANKS
    group = NW * RANKS
    early = n - group

    def gone(block):
        return jnp.where(block[:, 0:128].astype(F32)[:, 0:1] > 64.0, NEG, 0.0)

    def score(k, _):
        every = mem[k, 0:NZ - 1].reshape(early, feat)
        s = dot_t(every, every) + gone(every)
        s = jnp.where(iota((early, early), 0) == iota((early, early), 1), NEG, s)
        near[k, :, 0:early] = jnp.max(s, axis=0, keepdims=True)
        return 0

    lax.fori_loop(0, 4, score, 0)
    collect(NZ - 1)

    xbuf[gx] = jnp.zeros((8, feat), F32)
    for k in range(4):
        xbuf[gx, k:k + 1, :] = acc[k, 0:1, :]
    top = jnp.max(jnp.max(flags[...], axis=0, keepdims=True), axis=1, keepdims=True)
    xbuf[gx, 4:5, :] = jnp.broadcast_to(jnp.where(top > 1.5 * MARK, 1.0, 0.0), (1, feat))

    def x_copy(k, place):
        return pltpu.make_async_remote_copy(
            src_ref=xbuf.at[gx], dst_ref=xbuf.at[place], send_sem=xss.at[k], recv_sem=xrs.at[k],
            device_id={"group": lax.rem(gx + k, NX)}, device_id_type=MESH)

    for k in range(1, NX):
        x_copy(k, gx).start()

    def score_last(k, _):
        every = mem[k].reshape(n, feat)
        last = every[early:]
        s = dot_t(every, last) + gone(every)
        s = jnp.where(iota((n, group), 0) == early + iota((n, group), 1), NEG, s)
        near[k, :, early:n] = jnp.max(s, axis=0, keepdims=True)
        s = dot_t(last, every[0:early]) + gone(last)
        near[k, :, 0:early] = jnp.maximum(near[k, :, 0:early], jnp.max(s, axis=0, keepdims=True))
        return 0

    lax.fori_loop(0, 4, score_last, 0)

    for k in range(1, NX):
        x_copy(k, lax.rem(gx - k + NX, NX)).wait_recv()
    totals = ((xbuf[0] + xbuf[1]) + xbuf[2]) + xbuf[3]
    centroids = totals * lax.rsqrt(jnp.mean(totals * totals, axis=-1, keepdims=True) + EPS)
    cent_o[...] = centroids[0:4]
    flag_o[...] = jnp.broadcast_to(totals[4:5, 0:128], (8, 128))
    lowc = jnp.concatenate([centroids, centroids], axis=0).astype(BF16)
    for k in range(4):
        central = dot_t(lowc, mem[k].reshape(n, feat)) * (1.0 / feat)
        nearest = jnp.maximum(near[k] * (1.0 / feat), -1.0)
        for j in range(NZ):
            ret[j, k:k + 1, :] = nearest[:, j * 128:(j + 1) * 128]
            ret[j, 4 + k:5 + k, :] = central[k:k + 1, j * 128:(j + 1) * 128]

    def r_copy(j):
        return pltpu.make_async_remote_copy(
            src_ref=ret.at[j], dst_ref=rz.at[j], send_sem=rss.at[j], recv_sem=rrs.at[j],
            device_id={"owner": z_dev(j, -1)}, device_id_type=MESH)

    def p_copy(e):
        return pltpu.make_async_remote_copy(
            src_ref=pk.at[e], dst_ref=rp.at[e], send_sem=pss.at[e], recv_sem=prs.at[e],
            device_id={"owner": w_dev(e, -1)}, device_id_type=MESH)

    for j in range(1, NZ):
        r_copy(j).start()
    rz[0] = ret[0]
    rp[NW:] = jnp.zeros((NW, 8, 128), F32)
    for j in range(1, NZ):
        r_copy(j).wait_recv()
    got = [rz[j] for j in range(NZ)]
    block = iota((8, 128), 1) >> 4
    for e in range(NW):
        out = jnp.zeros((8, 128), F32)
        for j in range(NZ):
            shift = (j - e) % NZ * RANKS
            out = jnp.where(block == j, pltpu.roll(got[j], shift, 1) if shift else got[j], out)
        if e == 0:
            rp[0] = out
        else:
            pk[e] = out
            p_copy(e).start()
    for e in range(1, NW):
        p_copy(e).wait_recv()

    back = rp[...].reshape(128, 128).T
    high = back.astype(BF16)
    both = jnp.concatenate([high, (back - high.astype(F32)).astype(BF16)], axis=0)
    lane = (info[0:1, :].astype(I32) >> 5) * RANKS + info[1:2, :].astype(I32)
    mine = iota((128, rows), 0) == lane
    for table, out_ref in ((on_s, near_o), (oc_s, central_o)):
        took = dot(both, table[...])
        took = jnp.sum(jnp.where(mine, took[0:128] + took[128:256], 0.0), axis=0, keepdims=True)
        for k in range(rows // 128):
            out_ref[k:k + 1, :] = took[:, k * 128:(k + 1) * 128]

    for j in range(1, NZ):
        m_copy(j).wait_send()
        for f in range(HALVES):
            z_copy(j, f).wait_send()
        r_copy(j).wait_send()
    for e in range(1, NW):
        p_copy(e).wait_send()
    for k in range(1, NX):
        x_copy(k, gx).wait_send()

    def drain(j, _):
        for e in range(1, NW):
            for f in range(HALVES):
                i_copy(j, f, e).wait_send()
        return 0

    lax.fori_loop(0, NZ, drain, 0)


def window(cap, collective_id, embeddings, ids, home_map):
    rows, feat = embeddings.shape
    dma = pltpu.SemaphoreType.DMA
    lanes = -(-cap // 128) * 128
    vmem = pl.BlockSpec(memory_space=pltpu.VMEM)
    cent, near, central, flag = pl.pallas_call(
        functools.partial(kernel, cap),
        out_shape=(
            jax.ShapeDtypeStruct((4, feat), F32),
            jax.ShapeDtypeStruct((rows // 128, 128), F32),
            jax.ShapeDtypeStruct((rows // 128, 128), F32),
            jax.ShapeDtypeStruct((8, 128), F32),
        ),
        in_specs=[pl.BlockSpec(memory_space=pl.ANY), vmem, vmem],
        out_specs=(vmem,) * 4,
        scratch_shapes=[
            pltpu.VMEM((rows, feat), BF16),
            pltpu.VMEM((2 * NZ, HALVES, cap, feat // HALVES), BF16),
            pltpu.VMEM((2 * NZ, 8, lanes), F32),
            pltpu.VMEM((NZ, HALVES, NW, 4, RANKS, feat // HALVES), BF16),
            pltpu.VMEM((4, NZ, NW, RANKS, feat), BF16),
            pltpu.VMEM((8, rows), F32),
            pltpu.VMEM((16, rows), BF16),
            pltpu.VMEM((4, 16, feat), F32),
            pltpu.VMEM((16, 128), F32),
            pltpu.VMEM((NX, 8, feat), F32),
            pltpu.VMEM((4, 1, NZ * NW * RANKS), F32),
            pltpu.VMEM((NZ, 8, 128), F32),
            pltpu.VMEM((NZ, 8, 128), F32),
            pltpu.VMEM((NW, 8, 128), F32),
            pltpu.VMEM((2 * NW, 8, 128), F32),
            pltpu.VMEM((128, rows), BF16),
            pltpu.VMEM((128, rows), BF16),
            dma, dma((NZ, HALVES)), dma((NZ, HALVES)), dma((NZ,)), dma((NZ,)),
            dma((NZ, HALVES, NW)), dma((NZ, HALVES, NW)),
            dma((NX,)), dma((NX,)), dma((NZ,)), dma((NZ,)), dma((NW,)), dma((NW,)),
        ],
        compiler_params=pltpu.CompilerParams(
            collective_id=collective_id, has_side_effects=True, vmem_limit_bytes=62 * 1024 * 1024),
    )(embeddings, ids, home_map)
    return cent, near.reshape(-1), central.reshape(-1), flag


def body(embeddings, assignment, home_map):
    ids = assignment.reshape(1, -1)
    table = home_map.reshape(1, -1)
    cent, near, central, flag = window(CAP, 0, embeddings, ids, table)
    return lax.cond(
        flag[0, 0] > 0.5,
        lambda e, i, t, *_: window(PLANE * 12, 1, e, i, t)[:3],
        lambda e, i, t, *done: done,
        embeddings, ids, table, cent, near, central)


def solution(mesh):
    in_specs = (P(("group", "owner"), None), P(("group", "owner"), None), P())
    out_specs = (P("owner", None), P(("group", "owner")), P(("group", "owner")))
    return jax.shard_map(body, mesh=mesh, in_specs=in_specs, out_specs=out_specs, check_vma=False)
```

```python
import functools

import jax
import jax.numpy as jnp
from jax import lax
from jax.experimental import pallas as pl
from jax.experimental.pallas import tpu as pltpu
from jax.sharding import PartitionSpec as P

MESH = pl.DeviceIdType.MESH
F32 = jnp.float32
BF16 = jnp.bfloat16
I32 = jnp.int32

NZ, NY, NC = 8, 4, 2
NW = NY * NC
NX = 4
PLANE = 32
RANKS = 16
MARK = 128.0
NEG = -1e30
EPS = 1e-06
HALVES = 2
CAP = 272


def dot(a, b):
    return lax.dot_general(a, b, (((1,), (0,)), ((), ())), preferred_element_type=F32)


def dot_t(a, b):
    return lax.dot_general(a, b, (((1,), (1,)), ((), ())), preferred_element_type=F32)


def iota(shape, axis):
    return lax.broadcasted_iota(I32, shape, axis)


def hot(mask):
    return jnp.where(mask, 1.0, 0.0).astype(BF16)


def z_of(j):
    return jnp.where(lax.rem(j, 2) == 1, (j + 1) // 2, NZ - j // 2)


def kernel(cap, emb_hbm, ids, hm, cent_o, near_o, central_o, flag_o,
           emb, cent_v, near_v, central_v, head, spr, sel, buf, meta, stage, mem, info, val, acc, flags, xbuf, near, ret, rz, pk, rp, on_s, oc_s,
           esem, osem, zss, zrs, mss, mrs, iss, irs, xss, xrs, rss, rrs, pss, prs):
    rows, feat = emb.shape
    half = feat // HALVES
    clusters = hm.shape[1]
    gx = lax.axis_index("group")
    me = lax.axis_index("owner")
    z, y, c = me // NW, lax.rem(me // NC, NY), lax.rem(me, NC)

    def z_dev(j, sign=1):
        return lax.rem(z + sign * z_of(j) + NZ, NZ) * NW + y * NC + c

    def w_dev(e, sign):
        dy, dc = e // NC, lax.rem(e, NC)
        return z * NW + lax.rem(y + sign * dy + NY, NY) * NC + lax.rem(c + dc, NC)

    barrier = pltpu.get_barrier_semaphore()
    for j in range(1, NZ):
        pl.semaphore_signal(barrier, inc=1, device_id={"owner": z_dev(j)}, device_id_type=MESH)
    for e in range(1, NW):
        pl.semaphore_signal(barrier, inc=1, device_id={"owner": w_dev(e, 1)}, device_id_type=MESH)
    for k in range(1, NX):
        pl.semaphore_signal(barrier, inc=1, device_id={"group": lax.rem(gx + k, NX)}, device_id_type=MESH)
    load = pltpu.make_async_copy(emb_hbm, emb, esem)
    load.start()

    h = hm[...]
    dz = ((h >> 5) - z) & (NZ - 1)
    jz = jnp.where(dz == 0, 0, jnp.where(dz <= NZ // 2, 2 * dz - 1, 2 * (NZ - dz)))
    rel = (jz << 5) + ((((h >> 3) - y) & (NY - 1)) << 3) + ((((h >> 2) - c) & 1) << 2) + (h & 3)
    perm = hot(iota((clusters, clusters), 0) == rel)
    home = dot(perm, hot(iota((clusters, rows), 0) == ids[...])).astype(BF16)
    before = hot(iota((256, 256), 0) < iota((256, 256), 1))
    same = hot((iota((clusters, clusters), 0) >> 5) == (iota((clusters, clusters), 1) >> 5))
    base = jnp.zeros((clusters, 1), F32)
    number = iota((clusters, 256), 0).astype(F32)
    for k in range(rows // 256):
        part = home[:, k * 256:(k + 1) * 256]
        count = dot(part, before) + base
        wide = part.astype(F32)
        lanes = pl.ds(k * 256, 256)
        info[0:1, lanes] = jnp.sum(wide * number, axis=0, keepdims=True)
        info[1:2, lanes] = jnp.sum(wide * count, axis=0, keepdims=True)
        info[2:3, lanes] = jnp.sum(dot(same, part) * count, axis=0, keepdims=True)
        base = base + jnp.sum(wide, axis=1, keepdims=True)
    rel_home = info[0:1, :].astype(I32)
    rank = info[1:2, :]
    place = info[2:3, :]
    plane = rel_home >> 5
    e4 = rel_home & (PLANE - 1)
    irank = rank.astype(I32)
    own = (e4 & 3) < 3
    tile = (e4 >> 2) * 3 + jnp.where(own, e4 & 3, irank >> 2)
    row = jnp.where(own, irank, 12 + (irank & 3))
    info[3:4, :] = jnp.where(place < cap, plane * cap + place.astype(I32), -1).astype(F32)
    over = jnp.where(jnp.max(place, axis=1, keepdims=True) >= cap, 1.0, 0.0)
    row_of = iota((16, rows), 0)
    val[...] = jnp.where(row_of == 0, tile + 1, jnp.where(row_of == 1, row, 0)).astype(F32).astype(BF16)
    lanes = meta.shape[2]
    if lanes > cap:
        meta[0:NZ] = jnp.zeros((NZ, 8, lanes), F32)

    load.wait()

    def z_copy(j, f):
        return pltpu.make_async_remote_copy(
            src_ref=buf.at[j, f], dst_ref=buf.at[NZ + j, f], send_sem=zss.at[j, f], recv_sem=zrs.at[j, f],
            device_id={"owner": z_dev(j)}, device_id_type=MESH)

    def m_copy(j):
        return pltpu.make_async_remote_copy(
            src_ref=meta.at[j], dst_ref=meta.at[NZ + j], send_sem=mss.at[j], recv_sem=mrs.at[j],
            device_id={"owner": z_dev(j)}, device_id_type=MESH)

    def i_copy(j, f, e):
        return pltpu.make_async_remote_copy(
            src_ref=stage.at[j, f, e], dst_ref=mem.at[0:3, j, e, :, pl.ds(f * half, half)],
            send_sem=iss.at[j, f, e], recv_sem=irs.at[j, f, e],
            device_id={"owner": w_dev(e, 1)}, device_id_type=MESH)

    def send_plane(i, _):
        j = lax.rem(i + 1, NZ)
        pick = hot(iota((cap, rows), 0) + j * cap == info[3:4, :].astype(I32))
        x = dot(pick, emb[...])
        x = x * lax.rsqrt(jnp.mean(x * x, axis=-1, keepdims=True) + EPS)
        for f in range(HALVES):
            buf[j, f] = x[:, f * half:(f + 1) * half].astype(BF16)
        notes = dot_t(val[...], pick)[0:8]
        meta[j, :, 0:cap] = jnp.where(iota((8, cap), 0) == 2, over, notes)

        @pl.when(i == 0)
        def _():
            pl.semaphore_wait(barrier, NZ - 1 + NW - 1 + NX - 1)

        @pl.when(j > 0)
        def _():
            m_copy(j).start()
            for f in range(HALVES):
                z_copy(j, f).start()
        return 0

    lax.fori_loop(0, NZ, send_plane, 0)

    line = iota((128, 1), 0)
    v = line & 7
    code = (line >> 3) * 4
    low = info[0:1, :].astype(I32) & (PLANE - 1)
    on_s[...] = hot(jnp.where((v < 4) & (line < 64), code + v, -1) == low)
    oc_s[...] = hot(jnp.where((v >= 4) & (line < 64), code + v - 4, -1) == low)
    acc[...] = jnp.zeros_like(acc)
    flags[...] = jnp.zeros_like(flags)
    first = hot((iota((16, 128), 1) == 0))

    group = NW * RANKS
    to = iota((group, 3 * group), 0)
    at = iota((group, 3 * group), 1)
    sel[...] = hot(at == ((to & 15) >> 2) * group + (to & ~15) + 12 + (to & 3))

    def collect(j):
        for e in range(1, NW):
            for f in range(HALVES):
                i_copy(j, f, e).wait_recv()
        tiles = mem[0:3, j].reshape(3 * group, feat)
        mem[3, j] = dot(sel[...], tiles).astype(BF16).reshape(NW, RANKS, feat)
        used = (iota((16, group), 1) & 15) < 12
        for k in range(4):
            block = mem[k, j].reshape(group, feat)
            lead = dot_t(first, block[:, 0:128])
            flags[...] = jnp.maximum(flags[...], lead)
            acc[k] += dot(hot((lead < 64.0) & used), block)

    def spread(j, slot):
        notes = meta[slot]
        q = ((notes[0:1, 0:cap] - 1.0) * RANKS + notes[1:2, 0:cap]).astype(I32)
        mark = MARK + MARK * jnp.max(notes[2:3, 0:cap], axis=1, keepdims=True)
        wide = jnp.where(iota((NW * 48, cap), 0) == q, 1.0, 0.0)
        absent = 1.0 - jnp.sum(wide, axis=1, keepdims=True)
        head[...] = jnp.where(iota((NW * 48, 128), 1) == 0, absent * mark, 0.0)
        spr[...] = wide.astype(BF16)

    def piece(j, slot, f):
        out = dot(spr[...], buf[slot, f])
        if f == 0:
            stage[j, f, :, :, :, 0:128] = (out[:, 0:128] + head[...]).astype(BF16).reshape(NW, 3, RANKS, 128)
            stage[j, f, :, :, :, 128:] = out[:, 128:].astype(BF16).reshape(NW, 3, RANKS, half - 128)
        else:
            stage[j, f] = out.astype(BF16).reshape(NW, 3, RANKS, half)
        for e in range(1, NW):
            i_copy(j, f, e).start()
        mem[0:3, j, 0, :, f * half:(f + 1) * half] = stage[j, f, 0]

    def step(j, _):
        @pl.when(j > 0)
        def _():
            m_copy(j).wait_recv()
        slot = jnp.where(j == 0, 0, NZ + j)
        spread(j, slot)
        for f in range(HALVES):
            @pl.when(j > 0)
            def _():
                z_copy(j, f).wait_recv()
            piece(j, slot, f)

        @pl.when(j > 0)
        def _():
            collect(j - 1)
        return 0

    lax.fori_loop(0, NZ - 1, step, 0)

    n = NZ * group
    early = n - group

    def gone(block):
        empty = block[:, 0:128].astype(F32)[:, 0:1] > 64.0
        return jnp.where(empty | ((iota((block.shape[0], 1), 0) & 15) >= 12), NEG, 0.0)

    def score(k, _):
        every = mem[k, 0:NZ - 1].reshape(early, feat)
        s = dot_t(every, every) + gone(every)
        s = jnp.where(iota((early, early), 0) == iota((early, early), 1), NEG, s)
        near[k, :, 0:early] = jnp.max(s, axis=0, keepdims=True)
        return 0

    last_j = NZ - 1
    m_copy(last_j).wait_recv()
    spread(last_j, NZ + last_j)
    for f in range(HALVES):
        if f == HALVES - 1:
            collect(last_j - 1)
            lax.fori_loop(0, 2, score, 0)
        z_copy(last_j, f).wait_recv()
        piece(last_j, NZ + last_j, f)
    lax.fori_loop(2, 4, score, 0)
    collect(last_j)

    xbuf[gx] = jnp.zeros((8, feat), F32)
    for k in range(4):
        xbuf[gx, k:k + 1, :] = acc[k, 0:1, :]
    top = jnp.max(jnp.max(flags[...], axis=0, keepdims=True), axis=1, keepdims=True)
    xbuf[gx, 4:5, :] = jnp.broadcast_to(jnp.where(top > 1.5 * MARK, 1.0, 0.0), (1, feat))

    def x_copy(k, place):
        return pltpu.make_async_remote_copy(
            src_ref=xbuf.at[gx], dst_ref=xbuf.at[place], send_sem=xss.at[k], recv_sem=xrs.at[k],
            device_id={"group": lax.rem(gx + k, NX)}, device_id_type=MESH)

    for k in range(1, NX):
        x_copy(k, gx).start()

    def score_last(k, _):
        every = mem[k].reshape(n, feat)
        last = every[early:]
        s = dot_t(every, last) + gone(every)
        s = jnp.where(iota((n, group), 0) == early + iota((n, group), 1), NEG, s)
        near[k, :, early:n] = jnp.max(s, axis=0, keepdims=True)
        s = dot_t(last, every[0:early]) + gone(last)
        near[k, :, 0:early] = jnp.maximum(near[k, :, 0:early], jnp.max(s, axis=0, keepdims=True))
        return 0

    lax.fori_loop(0, 4, score_last, 0)

    for k in range(1, NX):
        x_copy(k, lax.rem(gx - k + NX, NX)).wait_recv()
    totals = ((xbuf[0] + xbuf[1]) + xbuf[2]) + xbuf[3]
    centroids = totals * lax.rsqrt(jnp.mean(totals * totals, axis=-1, keepdims=True) + EPS)
    cent_v[...] = centroids[0:4]
    cent_out = pltpu.make_async_copy(cent_v, cent_o, osem.at[0])
    cent_out.start()
    flag_o[0, 0] = jnp.max(totals[4:5, 0:128]).astype(I32)
    lowc = jnp.concatenate([centroids, centroids], axis=0).astype(BF16)
    for k in range(4):
        central = dot_t(lowc, mem[k].reshape(n, feat)) * (1.0 / feat)
        nearest = jnp.maximum(near[k] * (1.0 / feat), -1.0)
        for j in range(NZ):
            ret[j, k:k + 1, :] = nearest[:, j * 128:(j + 1) * 128]
            ret[j, 4 + k:5 + k, :] = central[k:k + 1, j * 128:(j + 1) * 128]

    def r_copy(j):
        return pltpu.make_async_remote_copy(
            src_ref=ret.at[j], dst_ref=rz.at[j], send_sem=rss.at[j], recv_sem=rrs.at[j],
            device_id={"owner": z_dev(j, -1)}, device_id_type=MESH)

    def p_copy(e):
        return pltpu.make_async_remote_copy(
            src_ref=pk.at[e], dst_ref=rp.at[e], send_sem=pss.at[e], recv_sem=prs.at[e],
            device_id={"owner": w_dev(e, -1)}, device_id_type=MESH)

    for j in range(1, NZ):
        r_copy(j).start()
    rz[0] = ret[0]
    rp[NW:] = jnp.zeros((NW, 8, 128), F32)
    for j in range(1, NZ):
        r_copy(j).wait_recv()
    got = [rz[j] for j in range(NZ)]
    block = iota((8, 128), 1) >> 4
    for e in range(NW):
        out = jnp.zeros((8, 128), F32)
        for j in range(NZ):
            shift = (j - e) % NZ * RANKS
            out = jnp.where(block == j, pltpu.roll(got[j], shift, 1) if shift else got[j], out)
        if e == 0:
            rp[0] = out
        else:
            pk[e] = out
            p_copy(e).start()
    for e in range(1, NW):
        p_copy(e).wait_recv()

    back = rp[...].reshape(128, 128).T
    high = back.astype(BF16)
    both = jnp.concatenate([high, (back - high.astype(F32)).astype(BF16)], axis=0)
    lane = (info[0:1, :].astype(I32) >> 5) * RANKS + info[1:2, :].astype(I32)
    mine = iota((128, rows), 0) == lane
    outs = [cent_out]
    for table, out_v, out_ref in ((on_s, near_v, near_o), (oc_s, central_v, central_o)):
        took = dot(both, table[...])
        took = jnp.sum(jnp.where(mine, took[0:128] + took[128:256], 0.0), axis=0, keepdims=True)
        for k in range(rows // 128):
            out_v[k:k + 1, :] = took[:, k * 128:(k + 1) * 128]
        outs.append(pltpu.make_async_copy(out_v, out_ref, osem.at[len(outs)]))
        outs[-1].start()

    for j in range(1, NZ):
        m_copy(j).wait_send()
        for f in range(HALVES):
            z_copy(j, f).wait_send()
        r_copy(j).wait_send()
    for e in range(1, NW):
        p_copy(e).wait_send()
    for k in range(1, NX):
        x_copy(k, gx).wait_send()

    def drain(j, _):
        for e in range(1, NW):
            for f in range(HALVES):
                i_copy(j, f, e).wait_send()
        return 0

    lax.fori_loop(0, NZ, drain, 0)
    for out in outs:
        out.wait()


def window(cap, collective_id, embeddings, ids, home_map):
    rows, feat = embeddings.shape
    dma = pltpu.SemaphoreType.DMA
    lanes = -(-cap // 128) * 128
    vmem = pl.BlockSpec(memory_space=pltpu.VMEM)
    cent, near, central, flag = pl.pallas_call(
        functools.partial(kernel, cap),
        out_shape=(
            jax.ShapeDtypeStruct((4, feat), F32),
            jax.ShapeDtypeStruct((rows // 128, 128), F32),
            jax.ShapeDtypeStruct((rows // 128, 128), F32),
            jax.ShapeDtypeStruct((1, 1), I32),
        ),
        in_specs=[pl.BlockSpec(memory_space=pl.ANY), vmem, vmem],
        out_specs=(pl.BlockSpec(memory_space=pltpu.HBM),) * 3 + (pl.BlockSpec(memory_space=pltpu.SMEM),),
        scratch_shapes=[
            pltpu.VMEM((rows, feat), BF16),
            pltpu.VMEM((4, feat), F32),
            pltpu.VMEM((rows // 128, 128), F32),
            pltpu.VMEM((rows // 128, 128), F32),
            pltpu.VMEM((NW * 48, 128), F32),
            pltpu.VMEM((NW * 48, cap), BF16),
            pltpu.VMEM((NW * RANKS, 3 * NW * RANKS), BF16),
            pltpu.VMEM((2 * NZ, HALVES, cap, feat // HALVES), BF16),
            pltpu.VMEM((2 * NZ, 8, lanes), F32),
            pltpu.VMEM((NZ, HALVES, NW, 3, RANKS, feat // HALVES), BF16),
            pltpu.VMEM((4, NZ, NW, RANKS, feat), BF16),
            pltpu.VMEM((8, rows), F32),
            pltpu.VMEM((16, rows), BF16),
            pltpu.VMEM((4, 16, feat), F32),
            pltpu.VMEM((16, 128), F32),
            pltpu.VMEM((NX, 8, feat), F32),
            pltpu.VMEM((4, 1, NZ * NW * RANKS), F32),
            pltpu.VMEM((NZ, 8, 128), F32),
            pltpu.VMEM((NZ, 8, 128), F32),
            pltpu.VMEM((NW, 8, 128), F32),
            pltpu.VMEM((2 * NW, 8, 128), F32),
            pltpu.VMEM((128, rows), BF16),
            pltpu.VMEM((128, rows), BF16),
            dma, dma((3,)), dma((NZ, HALVES)), dma((NZ, HALVES)), dma((NZ,)), dma((NZ,)),
            dma((NZ, HALVES, NW)), dma((NZ, HALVES, NW)),
            dma((NX,)), dma((NX,)), dma((NZ,)), dma((NZ,)), dma((NW,)), dma((NW,)),
        ],
        compiler_params=pltpu.CompilerParams(
            collective_id=collective_id, has_side_effects=True, vmem_limit_bytes=62 * 1024 * 1024),
    )(embeddings, ids, home_map)
    return cent, near.reshape(-1), central.reshape(-1), flag


def body(embeddings, assignment, home_map):
    ids = assignment.reshape(1, -1)
    table = home_map.reshape(1, -1)
    cent, near, central, flag = window(CAP, 0, embeddings, ids, table)
    return lax.cond(
        flag.reshape(()) > 0,
        lambda e, i, t, *_: window(PLANE * 12, 1, e, i, t)[:3],
        lambda e, i, t, *done: done,
        embeddings, ids, table, cent, near, central)


def solution(mesh):
    in_specs = (P(("group", "owner"), None), P(("group", "owner"), None), P())
    out_specs = (P("owner", None), P(("group", "owner")), P(("group", "owner")))
    return jax.shard_map(body, mesh=mesh, in_specs=in_specs, out_specs=out_specs, check_vma=False)
```

```python
import functools

import jax
import jax.numpy as jnp
from jax import lax
from jax.experimental import pallas as pl
from jax.experimental.pallas import tpu as pltpu
from jax.sharding import PartitionSpec as P

MESH = pl.DeviceIdType.MESH
F32 = jnp.float32
BF16 = jnp.bfloat16
I32 = jnp.int32

NZ, NY, NC = 8, 4, 2
NW = NY * NC
NX = 4
PLANE = 32
RANKS = 16
MARK = 128.0
NEG = -1e30
EPS = 1e-06
CUTS = ((0, 512), (512, 512))
HALVES = len(CUTS)
CAP = 272


def dot(a, b):
    return lax.dot_general(a, b, (((1,), (0,)), ((), ())), preferred_element_type=F32)


def dot_t(a, b):
    return lax.dot_general(a, b, (((1,), (1,)), ((), ())), preferred_element_type=F32)


def iota(shape, axis):
    return lax.broadcasted_iota(I32, shape, axis)


def hot(mask):
    return jnp.where(mask, 1.0, 0.0).astype(BF16)


def z_of(j):
    return jnp.where(lax.rem(j, 2) == 1, (j + 1) // 2, NZ - j // 2)


def kernel(cap, emb_hbm, ids, hm, cent_o, near_o, central_o, flag_o,
           emb, leads, head, spr, sel, buf, meta, stage, mem, info, val, acc, flags, xbuf, near, ret, rz, pk, rp, on_s, oc_s,
           esem, zss, zrs, mss, mrs, iss, irs, xss, xrs, rss, rrs, pss, prs):
    rows, feat = emb.shape
    clusters = hm.shape[1]
    gx = lax.axis_index("group")
    me = lax.axis_index("owner")
    z, y, c = me // NW, lax.rem(me // NC, NY), lax.rem(me, NC)

    def z_dev(j, sign=1):
        return lax.rem(z + sign * z_of(j) + NZ, NZ) * NW + y * NC + c

    def w_dev(e, sign):
        dy, dc = e // NC, lax.rem(e, NC)
        return z * NW + lax.rem(y + sign * dy + NY, NY) * NC + lax.rem(c + dc, NC)

    barrier = pltpu.get_barrier_semaphore()
    for j in range(1, NZ):
        pl.semaphore_signal(barrier, inc=1, device_id={"owner": z_dev(j)}, device_id_type=MESH)
    for e in range(1, NW):
        pl.semaphore_signal(barrier, inc=1, device_id={"owner": w_dev(e, 1)}, device_id_type=MESH)
    for k in range(1, NX):
        pl.semaphore_signal(barrier, inc=1, device_id={"group": lax.rem(gx + k, NX)}, device_id_type=MESH)
    load = pltpu.make_async_copy(emb_hbm, emb, esem)
    load.start()

    h = hm[...]
    dz = ((h >> 5) - z) & (NZ - 1)
    jz = jnp.where(dz == 0, 0, jnp.where(dz <= NZ // 2, 2 * dz - 1, 2 * (NZ - dz)))
    rel = (jz << 5) + ((((h >> 3) - y) & (NY - 1)) << 3) + ((((h >> 2) - c) & 1) << 2) + (h & 3)
    perm = hot(iota((clusters, clusters), 0) == rel)
    home = dot(perm, hot(iota((clusters, rows), 0) == ids[...])).astype(BF16)
    before = hot(iota((256, 256), 0) < iota((256, 256), 1))
    same = hot((iota((clusters, clusters), 0) >> 5) == (iota((clusters, clusters), 1) >> 5))
    base = jnp.zeros((clusters, 1), F32)
    number = iota((clusters, 256), 0).astype(F32)
    for k in range(rows // 256):
        part = home[:, k * 256:(k + 1) * 256]
        count = dot(part, before) + base
        wide = part.astype(F32)
        lanes = pl.ds(k * 256, 256)
        info[0:1, lanes] = jnp.sum(wide * number, axis=0, keepdims=True)
        info[1:2, lanes] = jnp.sum(wide * count, axis=0, keepdims=True)
        info[2:3, lanes] = jnp.sum(dot(same, part) * count, axis=0, keepdims=True)
        base = base + jnp.sum(wide, axis=1, keepdims=True)
    rel_home = info[0:1, :].astype(I32)
    rank = info[1:2, :]
    place = info[2:3, :]
    plane = rel_home >> 5
    e4 = rel_home & (PLANE - 1)
    irank = rank.astype(I32)
    own = (e4 & 3) < 3
    tile = (e4 >> 2) * 3 + jnp.where(own, e4 & 3, irank >> 2)
    row = jnp.where(own, irank, 12 + (irank & 3))
    info[3:4, :] = jnp.where(place < cap, plane * cap + place.astype(I32), -1).astype(F32)
    over = jnp.where(jnp.max(place, axis=1, keepdims=True) >= cap, 1.0, 0.0)
    row_of = iota((16, rows), 0)
    val[...] = jnp.where(row_of == 0, tile + 1, jnp.where(row_of == 1, row, 0)).astype(F32).astype(BF16)
    lanes = meta.shape[2]
    if lanes > cap:
        meta[0:NZ] = jnp.zeros((NZ, 8, lanes), F32)

    load.wait()

    def z_copy(j, f):
        return pltpu.make_async_remote_copy(
            src_ref=buf.at[j, :, pl.ds(*CUTS[f])], dst_ref=buf.at[NZ + j, :, pl.ds(*CUTS[f])], send_sem=zss.at[j, f], recv_sem=zrs.at[j, f],
            device_id={"owner": z_dev(j)}, device_id_type=MESH)

    def m_copy(j):
        return pltpu.make_async_remote_copy(
            src_ref=meta.at[j], dst_ref=meta.at[NZ + j], send_sem=mss.at[j], recv_sem=mrs.at[j],
            device_id={"owner": z_dev(j)}, device_id_type=MESH)

    def i_copy(j, f, e):
        return pltpu.make_async_remote_copy(
            src_ref=stage.at[j, e, :, :, pl.ds(*CUTS[f])], dst_ref=mem.at[0:3, j, e, :, pl.ds(*CUTS[f])],
            send_sem=iss.at[j, f, e], recv_sem=irs.at[j, f, e],
            device_id={"owner": w_dev(e, 1)}, device_id_type=MESH)

    def send_plane(i, _):
        j = lax.rem(i + 1, NZ)
        pick = hot(iota((cap, rows), 0) + j * cap == info[3:4, :].astype(I32))
        x = dot(pick, emb[...])
        x = x * lax.rsqrt(jnp.mean(x * x, axis=-1, keepdims=True) + EPS)
        buf[j] = x.astype(BF16)
        notes = dot_t(val[...], pick)[0:8]
        meta[j, :, 0:cap] = jnp.where(iota((8, cap), 0) == 2, over, notes)

        @pl.when(i == 0)
        def _():
            pl.semaphore_wait(barrier, NZ - 1 + NW - 1 + NX - 1)

        @pl.when(j > 0)
        def _():
            m_copy(j).start()
            for f in range(HALVES):
                z_copy(j, f).start()
        return 0

    lax.fori_loop(0, NZ, send_plane, 0)

    line = iota((128, 1), 0)
    v = line & 7
    code = (line >> 3) * 4
    low = info[0:1, :].astype(I32) & (PLANE - 1)
    on_s[...] = hot(jnp.where((v < 4) & (line < 64), code + v, -1) == low)
    oc_s[...] = hot(jnp.where((v >= 4) & (line < 64), code + v - 4, -1) == low)
    acc[...] = jnp.zeros_like(acc)
    flags[...] = jnp.zeros_like(flags)
    first = hot((iota((16, 128), 1) == 0))

    group = NW * RANKS
    to = iota((group, 3 * group), 0)
    at = iota((group, 3 * group), 1)
    sel[...] = hot(at == ((to & 15) >> 2) * group + (to & ~15) + 12 + (to & 3))

    def collect(j):
        for e in range(1, NW):
            for f in range(HALVES):
                i_copy(j, f, e).wait_recv()
        tiles = mem[0:3, j].reshape(3 * group, feat)
        mem[3, j] = dot(sel[...], tiles).astype(BF16).reshape(NW, RANKS, feat)
        used = (iota((16, group), 1) & 15) < 12
        for k in range(4):
            block = mem[k, j].reshape(group, feat)
            lead = dot_t(first, block[:, 0:128])
            flags[...] = jnp.maximum(flags[...], lead)
            leads[k] = jnp.where((lead < 64.0) & used, 0.0, NEG)[0:1]
            acc[k] += dot(hot((lead < 64.0) & used), block)

    def spread(j, slot):
        notes = meta[slot]
        q = ((notes[0:1, 0:cap] - 1.0) * RANKS + notes[1:2, 0:cap]).astype(I32)
        mark = MARK + MARK * jnp.max(notes[2:3, 0:cap], axis=1, keepdims=True)
        wide = jnp.where(iota((NW * 48, cap), 0) == q, 1.0, 0.0)
        absent = 1.0 - jnp.sum(wide, axis=1, keepdims=True)
        head[...] = jnp.where(iota((NW * 48, 128), 1) == 0, absent * mark, 0.0)
        spr[...] = wide.astype(BF16)

    def piece(j, slot, f):
        lo, wide = CUTS[f]
        out = dot(spr[...], buf[slot, :, lo:lo + wide])
        if f == 0:
            first_lanes = (out[:, 0:128] + head[...]).astype(BF16)
            stage[j, :, :, :, 0:128] = first_lanes.reshape(NW, 3, RANKS, 128)
            stage[j, :, :, :, 128:wide] = out[:, 128:].astype(BF16).reshape(NW, 3, RANKS, wide - 128)
        else:
            stage[j, :, :, :, lo:lo + wide] = out.astype(BF16).reshape(NW, 3, RANKS, wide)
        for e in (4, 5, 2, 6, 3, 7, 1):
            i_copy(j, f, e).start()
        mem[0:3, j, 0, :, lo:lo + wide] = stage[j, 0, :, :, lo:lo + wide]

    def step(j, _):
        @pl.when(j > 0)
        def _():
            m_copy(j).wait_recv()
        slot = jnp.where(j == 0, 0, NZ + j)
        spread(j, slot)
        for f in range(HALVES):
            @pl.when(j > 0)
            def _():
                z_copy(j, f).wait_recv()
            piece(j, slot, f)

        @pl.when(j > 0)
        def _():
            collect(j - 1)
        return 0

    lax.fori_loop(0, NZ - 1, step, 0)

    n = NZ * group
    early = n - group

    def gone(block):
        empty = block[:, 0:128].astype(F32)[:, 0:1] > 64.0
        return jnp.where(empty | ((iota((block.shape[0], 1), 0) & 15) >= 12), NEG, 0.0)

    def score(k, _):
        every = mem[k, 0:NZ - 1].reshape(early, feat)
        s = dot_t(every, every) + gone(every)
        s = jnp.where(iota((early, early), 0) == iota((early, early), 1), NEG, s)
        near[k, :, 0:early] = jnp.max(s, axis=0, keepdims=True)
        return 0

    last_j = NZ - 1
    m_copy(last_j).wait_recv()
    spread(last_j, NZ + last_j)
    for f in range(HALVES):
        if f == HALVES - 1:
            collect(last_j - 1)
            lax.fori_loop(0, 2, score, 0)
        z_copy(last_j, f).wait_recv()
        piece(last_j, NZ + last_j, f)
    lax.fori_loop(2, 4, score, 0)
    collect(last_j)

    xbuf[gx] = jnp.zeros((8, feat), F32)
    for k in range(4):
        xbuf[gx, k:k + 1, :] = acc[k, 0:1, :]
    top = jnp.max(jnp.max(flags[...], axis=0, keepdims=True), axis=1, keepdims=True)
    xbuf[gx, 4:5, :] = jnp.broadcast_to(jnp.where(top > 1.5 * MARK, 1.0, 0.0), (1, feat))

    def x_copy(k, place):
        return pltpu.make_async_remote_copy(
            src_ref=xbuf.at[gx], dst_ref=xbuf.at[place], send_sem=xss.at[k], recv_sem=xrs.at[k],
            device_id={"group": lax.rem(gx + k, NX)}, device_id_type=MESH)

    for k in range(1, NX):
        x_copy(k, gx).start()

    def score_last(k, _):
        every = mem[k].reshape(n, feat)
        last = every[early:]
        both = dot_t(every, last)
        s = jnp.where(iota((n, group), 0) == early + iota((n, group), 1), NEG, both + gone(every))
        near[k, :, early:n] = jnp.max(s, axis=0, keepdims=True)
        best = jnp.max(both[0:early] + leads[k], axis=1, keepdims=True)
        diagonal = iota((group, group), 0) == iota((group, group), 1)
        for i in range(NZ - 1):
            part = jnp.where(diagonal, best[i * group:(i + 1) * group], NEG)
            lanes = pl.ds(i * group, group)
            near[k, :, lanes] = jnp.maximum(near[k, :, lanes], jnp.max(part, axis=0, keepdims=True))
        return 0

    lax.fori_loop(0, 4, score_last, 0)

    for k in range(1, NX):
        x_copy(k, lax.rem(gx - k + NX, NX)).wait_recv()
    totals = ((xbuf[0] + xbuf[1]) + xbuf[2]) + xbuf[3]
    centroids = totals * lax.rsqrt(jnp.mean(totals * totals, axis=-1, keepdims=True) + EPS)
    cent_o[...] = centroids[0:4]
    flag_o[0, 0] = jnp.max(totals[4:5, 0:128]).astype(I32)
    lowc = jnp.concatenate([centroids, centroids], axis=0).astype(BF16)
    for k in range(4):
        central = dot_t(lowc, mem[k].reshape(n, feat)) * (1.0 / feat)
        nearest = jnp.maximum(near[k] * (1.0 / feat), -1.0)
        for j in range(NZ):
            ret[j, k:k + 1, :] = nearest[:, j * 128:(j + 1) * 128]
            ret[j, 4 + k:5 + k, :] = central[k:k + 1, j * 128:(j + 1) * 128]

    def r_copy(j):
        return pltpu.make_async_remote_copy(
            src_ref=ret.at[j], dst_ref=rz.at[j], send_sem=rss.at[j], recv_sem=rrs.at[j],
            device_id={"owner": z_dev(j, -1)}, device_id_type=MESH)

    def p_copy(e):
        return pltpu.make_async_remote_copy(
            src_ref=pk.at[e], dst_ref=rp.at[e], send_sem=pss.at[e], recv_sem=prs.at[e],
            device_id={"owner": w_dev(e, -1)}, device_id_type=MESH)

    for j in range(1, NZ):
        r_copy(j).start()
    rz[0] = ret[0]
    rp[NW:] = jnp.zeros((NW, 8, 128), F32)
    for j in range(1, NZ):
        r_copy(j).wait_recv()
    got = [rz[j] for j in range(NZ)]
    block = iota((8, 128), 1) >> 4
    for e in range(NW):
        out = jnp.zeros((8, 128), F32)
        for j in range(NZ):
            shift = (j - e) % NZ * RANKS
            out = jnp.where(block == j, pltpu.roll(got[j], shift, 1) if shift else got[j], out)
        if e == 0:
            rp[0] = out
        else:
            pk[e] = out
            p_copy(e).start()
    for e in range(1, NW):
        p_copy(e).wait_recv()

    back = rp[...].reshape(128, 128).T
    high = back.astype(BF16)
    both = jnp.concatenate([high, (back - high.astype(F32)).astype(BF16)], axis=0)
    lane = (info[0:1, :].astype(I32) >> 5) * RANKS + info[1:2, :].astype(I32)
    mine = iota((128, rows), 0) == lane
    for table, out_ref in ((on_s, near_o), (oc_s, central_o)):
        took = dot(both, table[...])
        took = jnp.sum(jnp.where(mine, took[0:128] + took[128:256], 0.0), axis=0, keepdims=True)
        for k in range(rows // 128):
            out_ref[k:k + 1, :] = took[:, k * 128:(k + 1) * 128]

    for j in range(1, NZ):
        m_copy(j).wait_send()
        for f in range(HALVES):
            z_copy(j, f).wait_send()
        r_copy(j).wait_send()
    for e in range(1, NW):
        p_copy(e).wait_send()
    for k in range(1, NX):
        x_copy(k, gx).wait_send()

    def drain(j, _):
        for e in range(1, NW):
            for f in range(HALVES):
                i_copy(j, f, e).wait_send()
        return 0

    lax.fori_loop(0, NZ, drain, 0)


def window(cap, collective_id, embeddings, ids, home_map):
    rows, feat = embeddings.shape
    dma = pltpu.SemaphoreType.DMA
    lanes = -(-cap // 128) * 128
    vmem = pl.BlockSpec(memory_space=pltpu.VMEM)
    cent, near, central, flag = pl.pallas_call(
        functools.partial(kernel, cap),
        out_shape=(
            jax.ShapeDtypeStruct((4, feat), F32),
            jax.ShapeDtypeStruct((rows // 128, 128), F32),
            jax.ShapeDtypeStruct((rows // 128, 128), F32),
            jax.ShapeDtypeStruct((1, 1), I32),
        ),
        in_specs=[pl.BlockSpec(memory_space=pl.ANY), vmem, vmem],
        out_specs=(vmem,) * 3 + (pl.BlockSpec(memory_space=pltpu.SMEM),),
        scratch_shapes=[
            pltpu.VMEM((rows, feat), BF16),
            pltpu.VMEM((4, 1, NW * RANKS), F32),
            pltpu.VMEM((NW * 48, 128), F32),
            pltpu.VMEM((NW * 48, cap), BF16),
            pltpu.VMEM((NW * RANKS, 3 * NW * RANKS), BF16),
            pltpu.VMEM((2 * NZ, cap, feat), BF16),
            pltpu.VMEM((2 * NZ, 8, lanes), F32),
            pltpu.VMEM((NZ, NW, 3, RANKS, feat), BF16),
            pltpu.VMEM((4, NZ, NW, RANKS, feat), BF16),
            pltpu.VMEM((8, rows), F32),
            pltpu.VMEM((16, rows), BF16),
            pltpu.VMEM((4, 16, feat), F32),
            pltpu.VMEM((16, 128), F32),
            pltpu.VMEM((NX, 8, feat), F32),
            pltpu.VMEM((4, 1, NZ * NW * RANKS), F32),
            pltpu.VMEM((NZ, 8, 128), F32),
            pltpu.VMEM((NZ, 8, 128), F32),
            pltpu.VMEM((NW, 8, 128), F32),
            pltpu.VMEM((2 * NW, 8, 128), F32),
            pltpu.VMEM((128, rows), BF16),
            pltpu.VMEM((128, rows), BF16),
            dma, dma((NZ, HALVES)), dma((NZ, HALVES)), dma((NZ,)), dma((NZ,)),
            dma((NZ, HALVES, NW)), dma((NZ, HALVES, NW)),
            dma((NX,)), dma((NX,)), dma((NZ,)), dma((NZ,)), dma((NW,)), dma((NW,)),
        ],
        compiler_params=pltpu.CompilerParams(
            collective_id=collective_id, has_side_effects=True, vmem_limit_bytes=62 * 1024 * 1024),
    )(embeddings, ids, home_map)
    return cent, near.reshape(-1), central.reshape(-1), flag


def body(embeddings, assignment, home_map):
    ids = assignment.reshape(1, -1)
    table = home_map.reshape(1, -1)
    cent, near, central, flag = window(CAP, 0, embeddings, ids, table)
    return lax.cond(
        flag.reshape(()) > 0,
        lambda e, i, t, *_: window(PLANE * 12, 1, e, i, t)[:3],
        lambda e, i, t, *done: done,
        embeddings, ids, table, cent, near, central)


def solution(mesh):
    in_specs = (P(("group", "owner"), None), P(("group", "owner"), None), P())
    out_specs = (P("owner", None), P(("group", "owner")), P(("group", "owner")))
    return jax.shard_map(body, mesh=mesh, in_specs=in_specs, out_specs=out_specs, check_vma=False)
```
